32 devices in a mesh: tok: 4 (over y, x), row: 8 (over z, core).
Axes of the slice: x: 2, y: 2, z: 4, core: 2. Of those that a mesh axis runs over, the one named last changes fastest.
Arguments:
- hidden: bfloat16 [768, 28672], P('tok', 'row'), may hold values from -6 to 6
- resid: bfloat16 [768, 8192], P('tok', 'row'), may hold values from -6 to 6
- down_in: bfloat16 [28672, 256], P('row'), may hold values from -0.03125 to 0.03125
- down_out: bfloat16 [256, 8192], P(None, 'row'), may hold values from -0.375 to 0.375
- up_weight: bfloat16 [8192, 28672], P('row', 'tok'), may hold values from -0.0625 to 0.0625
- start: bfloat16 [28672, 256], P('tok'), may hold values from -6 to 6
Outputs:
- left_basis: float32 [8192, 256], P('row')
- right_basis: float32 [28672, 256], P(('tok', 'row'))
- core: float32 [256, 256], replicated
The draws below stay inside these ranges and needn't reach their ends.
All inputs are finite; a program needn't handle non-finite values.
Results may differ from the reference program's by a relative error of at most 0.0004.
Values sent between devices are 32-bit elements; how exact they have to be, the bound alone decides.
A program may use at most 128 MiB of HBM per device.

```python
import math
import jax
import jax.numpy as jnp
from jax import lax

D = 8192
FF = 28672
FW = 28672
R = 256
RD = 256
ITERS = 2
TOKENS = 768


def rough_field(key, rows, cols):
    values = jax.random.normal(key, (rows, cols), jnp.float32)
    return jnp.clip(values, -6.0, 6.0).astype(jnp.bfloat16)


def draw_hidden(key, part):
    return rough_field(jax.random.fold_in(key, 11), TOKENS, FF)


def draw_resid(key, part):
    return rough_field(jax.random.fold_in(key, 23), TOKENS, D)


def steps_of(key, extent, cuts, low, largest):
    def one(dim, shards_of):
        heights = jax.random.uniform(jax.random.fold_in(jax.random.fold_in(key, 6), dim), (shards_of,), jnp.float32, low / len(cuts), largest / len(cuts))
        return jnp.repeat(jnp.exp(heights), extent[dim] // shards_of).reshape((-1,) + (1,) * (len(extent) - dim - 1))

    gain = one(*cuts[0])
    for cut in cuts[1:]:
        gain = gain * one(*cut)
    return gain


def bell_draw(stream_key, dims, spread, reach, cuts=(), held_as=jnp.bfloat16):
    factor_of = steps_of(stream_key, dims, cuts, -0.22, 0.18) if cuts else 1.0
    entries = jax.random.normal(stream_key, dims, jnp.float32) * spread * factor_of
    return jnp.minimum(jnp.maximum(entries, -reach), reach).astype(held_as)


def setup_inputs(seed: int = 0) -> dict:
    keys = jax.random.split(jax.random.key(seed), 7)
    return {
        "hidden": draw_hidden(jax.random.fold_in(keys[6], 71), 0),
        "resid": draw_resid(jax.random.fold_in(keys[6], 71), 0),
        "down_in": bell_draw(keys[2], (FF, RD), FF ** -0.5, 0.03125, ((0, 8),)),
        "down_out": bell_draw(keys[3], (RD, D), RD ** -0.5, 0.375, ((1, 8),)),
        "up_weight": bell_draw(keys[4], (D, FW), D ** -0.5, 0.0625, ((0, 8), (1, 4))),
        "start": bell_draw(keys[5], (FW, R), 1.0, 6.0, ((0, 4),)),
    }


HIGH = lax.Precision.HIGHEST

def orthonormal(block):
    inner = jnp.dot(block.T, block, precision=HIGH)
    lower = jnp.linalg.cholesky(inner)
    return jax.scipy.linalg.solve_triangular(lower, block.T, lower=True).T

def reference(hidden, resid, down_in, down_out, up_weight, start):
    code = jnp.dot(hidden.astype(jnp.float32), down_in.astype(jnp.float32), preferred_element_type=jnp.float32)
    act_full = resid.astype(jnp.float32) + jnp.dot(code, down_out.astype(jnp.float32), precision=HIGH)

    def whiten(block):
        return jnp.dot(act_full.T, jnp.dot(act_full, block, precision=HIGH), precision=HIGH) / TOKENS
    weight = up_weight.astype(jnp.float32)
    right = start.astype(jnp.float32)
    left = jnp.zeros((D, R), jnp.float32)
    back = jnp.zeros((D, R), jnp.float32)
    for step in range(ITERS):
        image = jnp.dot(weight, right, precision=HIGH)
        left = orthonormal(whiten(image))
        back = whiten(left)
        right = orthonormal(jnp.dot(weight.T, back, precision=HIGH))
    core = jnp.dot(back.T, jnp.dot(weight, right, precision=HIGH), precision=HIGH)
    return (math.sqrt(D) * left, math.sqrt(FW) * right, core)
```

```python
import math

import jax
import jax.numpy as jnp
from jax import lax
from jax.experimental import pallas as pl
from jax.experimental.pallas import tpu as pltpu
from jax.sharding import PartitionSpec as P

ITERS = 2
HIGH = lax.Precision.HIGHEST
F32 = jnp.float32
BF16 = jnp.bfloat16


def inner(first, second):
    return lax.dot_general(
        first, second, (((0,), (0,)), ((), ())), precision=HIGH, preferred_element_type=F32
    )


def outer(first, second):
    return lax.dot_general(
        first, second, (((1,), (1,)), ((), ())), precision=HIGH, preferred_element_type=F32
    )


def solve_lower(lower, block):
    return jax.scipy.linalg.solve_triangular(lower, block.T, lower=True).T


def activations(hidden, resid, down_in, down_out):
    partial_value = jnp.dot(hidden, down_in, preferred_element_type=F32)
    code = lax.psum(partial_value, "row")
    return resid.astype(F32) + jnp.dot(code, down_out.astype(F32), precision=HIGH)


def feature_space(hidden, resid, down_in, down_out, up_weight, start):
    act_full = activations(hidden, resid, down_in, down_out)
    total_tokens = act_full.shape[0] * lax.axis_size("tok")
    features = up_weight.shape[0] * lax.axis_size("row")
    columns = up_weight.shape[1] * lax.axis_size("tok")

    def whiten(block):
        applied = lax.psum(jnp.dot(act_full, block, precision=HIGH), "row")
        return lax.psum(inner(act_full, applied), "tok") / total_tokens

    weight = up_weight.astype(F32)
    right = start.astype(F32)
    for step in range(ITERS):
        image = lax.psum(jnp.dot(weight, right, precision=HIGH), "tok")
        target = whiten(image)
        lower = jnp.linalg.cholesky(lax.psum(inner(target, target), "row"))
        left = solve_lower(lower, target)
        back = whiten(left)
        share = lax.psum_scatter(inner(weight, back), "row", scatter_dimension=0, tiled=True)
        right_lower = jnp.linalg.cholesky(lax.psum(inner(share, share), ("tok", "row")))
        piece = solve_lower(right_lower, share)
        right = lax.all_gather(piece, "row", axis=0, tiled=True)
    core = lax.psum(inner(back, jnp.dot(weight, right, precision=HIGH)), ("tok", "row"))
    return (math.sqrt(features) * left, math.sqrt(columns) * piece, core)


def split_rows(block):
    first = lax.reduce_precision(block, 8, 7)
    rest = block - first
    second = lax.reduce_precision(rest, 8, 7)
    third = rest - second
    return first.astype(BF16), second.astype(BF16), third.astype(BF16)


def product_kernel(first_ref, second_ref, third_ref, weight_ref, out_ref):
    weight = weight_ref[...]
    total = jnp.dot(third_ref[...], weight, preferred_element_type=F32)
    total += jnp.dot(second_ref[...], weight, preferred_element_type=F32)
    total += jnp.dot(first_ref[...], weight, preferred_element_type=F32)
    out_ref[0] = total


def applied_blocks(parts, weight, blocks):
    tokens, depth = parts[0].shape
    width = weight.shape[1] // blocks
    whole = pl.BlockSpec((tokens, depth), lambda i: (0, 0))
    return pl.pallas_call(
        product_kernel,
        grid=(blocks,),
        in_specs=[whole, whole, whole, pl.BlockSpec((depth, width), lambda i: (0, i))],
        out_specs=pl.BlockSpec((1, tokens, width), lambda i: (i, 0, 0)),
        out_shape=jax.ShapeDtypeStruct((blocks, tokens, width), F32),
        compiler_params=pltpu.CompilerParams(vmem_limit_bytes=48 * 2**20),
        cost_estimate=pl.CostEstimate(
            flops=6 * tokens * depth * weight.shape[1],
            bytes_accessed=4 * tokens * weight.shape[1] + 2 * weight.size,
            transcendentals=0,
        ),
    )(*parts, weight)


def inverse_factor(table):
    size = table.shape[0]
    nb = 64
    eye = (
        lax.broadcasted_iota(jnp.int32, (nb, nb), 0) == lax.broadcasted_iota(jnp.int32, (nb, nb), 1)
    ).astype(F32)
    index = lax.broadcasted_iota(jnp.int32, (nb, 1), 0)
    for at in range(0, size, nb):
        work = jnp.concatenate([table[at : at + nb, at : at + nb], eye], axis=1)
        for j in range(nb):
            scale = lax.rsqrt(work[j : j + 1, j : j + 1])
            row = work[j : j + 1, :] * scale
            column = work[:, j : j + 1] * scale
            work = jnp.where(index == j, row, work - jnp.where(index < j, 0.0, column) * row)
        small = work[:, nb:]
        rows = jnp.dot(small, table[at : at + nb, :], precision=HIGH, preferred_element_type=F32)
        table[at : at + nb, :] = rows
        if at + nb < size:
            below = rows[:, at + nb : size]
            table[at + nb :, :] = table[at + nb :, :] - inner(below, rows)


def coefficient_kernel(gram_ref, square_ref, imaged_ref, left_ref, right_ref, core_ref, grams, now, table):
    tokens, size = imaged_ref.shape
    pltpu.sync_copy(gram_ref, grams.at[0])
    pltpu.sync_copy(square_ref, grams.at[1])
    now[...] = imaged_ref[...] / tokens
    eye = (
        lax.broadcasted_iota(jnp.int32, (size, size), 0)
        == lax.broadcasted_iota(jnp.int32, (size, size), 1)
    ).astype(F32)

    def one(i, carry):
        block = now[...]
        mapped = jnp.dot(grams[lax.rem(i, 2)], block, precision=HIGH, preferred_element_type=F32)
        table[:, :size] = inner(block, mapped)
        table[:, size:] = eye
        inverse_factor(table)
        inverse = table[:, size:]
        left_ref[...] = right_ref[...]
        right_ref[...] = outer(block, inverse)
        turned = outer(mapped, inverse)
        core_ref[...] = inner(block, turned)
        now[...] = turned / tokens
        return carry

    right_ref[...] = jnp.zeros_like(right_ref)
    lax.fori_loop(0, 2 * ITERS, one, 0)


def coefficients(gram, square, imaged):
    tokens, size = imaged.shape
    tall = jax.ShapeDtypeStruct((tokens, size), F32)
    vmem = pl.BlockSpec(memory_space=pltpu.VMEM)
    return pl.pallas_call(
        coefficient_kernel,
        in_specs=[pl.BlockSpec(memory_space=pl.ANY)] * 2 + [vmem],
        out_specs=[vmem] * 3,
        out_shape=[tall, tall, jax.ShapeDtypeStruct((size, size), F32)],
        scratch_shapes=[
            pltpu.VMEM((2, tokens, tokens), F32),
            pltpu.VMEM((tokens, size), F32),
            pltpu.VMEM((size, 2 * size), F32),
        ],
        compiler_params=pltpu.CompilerParams(vmem_limit_bytes=48 * 2**20),
    )(gram, square, imaged)


def token_space(hidden, resid, down_in, down_out, up_weight, start):
    blocks = lax.axis_size("row")
    tokens = hidden.shape[0] * lax.axis_size("tok")
    features = up_weight.shape[0] * blocks
    columns = up_weight.shape[1] * lax.axis_size("tok")
    width = up_weight.shape[1] // blocks
    own = lax.axis_index("row")

    code = lax.psum(jnp.dot(hidden, down_in, preferred_element_type=F32), "row")
    code = lax.all_gather(code, "tok", axis=0, tiled=True)
    base = lax.all_gather(resid.astype(F32), "tok", axis=0, tiled=True)
    acts = base + jnp.dot(code, down_out.astype(F32), precision=HIGH)
    gram = lax.psum(outer(acts, acts), "row")

    parts = split_rows(acts)
    chunk = 256 if tokens % 256 == 0 else tokens
    pieces = []
    for at in range(0, tokens, chunk):
        block = applied_blocks([p[at : at + chunk] for p in parts], up_weight, blocks)
        pieces.append(lax.psum_scatter(block, "row", scatter_dimension=0, tiled=True)[0])
    applied = jnp.concatenate(pieces, axis=0)

    begin = lax.dynamic_slice_in_dim(start, own * width, width, axis=0).astype(F32)
    sums = jnp.concatenate(
        [outer(applied, applied), jnp.dot(applied, begin, precision=HIGH)], axis=1
    )
    sums = lax.psum(sums, ("tok", "row"))
    square, imaged = sums[:, :tokens], sums[:, tokens:]

    left_coef, right_coef, core = coefficients(gram, square, imaged)
    left = inner(acts, left_coef)
    right = inner(applied, right_coef)
    return (math.sqrt(features) * left, math.sqrt(columns) * right, core)


def shards(hidden, *rest):
    tokens = hidden.shape[0] * lax.axis_size("tok")
    if tokens > 1024:
        return feature_space(hidden, *rest)
    return token_space(hidden, *rest)


def solution(mesh):
    placed = (
        P("tok", "row"),
        P("tok", "row"),
        P("row", None),
        P(None, "row"),
        P("row", "tok"),
        P("tok", None),
    )
    return jax.shard_map(
        shards,
        mesh=mesh,
        in_specs=placed,
        out_specs=(P("row", None), P(("tok", "row"), None), P()),
        check_vma=False,
    )
```

```python
import math

import jax
import jax.numpy as jnp
from jax import lax
from jax.experimental import pallas as pl
from jax.experimental.pallas import tpu as pltpu
from jax.sharding import PartitionSpec as P

ITERS = 2
HIGH = lax.Precision.HIGHEST
F32 = jnp.float32
BF16 = jnp.bfloat16


def inner(first, second):
    return lax.dot_general(
        first, second, (((0,), (0,)), ((), ())), precision=HIGH, preferred_element_type=F32
    )


def outer(first, second):
    return lax.dot_general(
        first, second, (((1,), (1,)), ((), ())), precision=HIGH, preferred_element_type=F32
    )


def solve_lower(lower, block):
    return jax.scipy.linalg.solve_triangular(lower, block.T, lower=True).T


def activations(hidden, resid, down_in, down_out):
    partial_value = jnp.dot(hidden, down_in, preferred_element_type=F32)
    code = lax.psum(partial_value, "row")
    return resid.astype(F32) + jnp.dot(code, down_out.astype(F32), precision=HIGH)


def feature_space(hidden, resid, down_in, down_out, up_weight, start):
    act_full = activations(hidden, resid, down_in, down_out)
    total_tokens = act_full.shape[0] * lax.axis_size("tok")
    features = up_weight.shape[0] * lax.axis_size("row")
    columns = up_weight.shape[1] * lax.axis_size("tok")

    def whiten(block):
        applied = lax.psum(jnp.dot(act_full, block, precision=HIGH), "row")
        return lax.psum(inner(act_full, applied), "tok") / total_tokens

    weight = up_weight.astype(F32)
    right = start.astype(F32)
    for step in range(ITERS):
        image = lax.psum(jnp.dot(weight, right, precision=HIGH), "tok")
        target = whiten(image)
        lower = jnp.linalg.cholesky(lax.psum(inner(target, target), "row"))
        left = solve_lower(lower, target)
        back = whiten(left)
        share = lax.psum_scatter(inner(weight, back), "row", scatter_dimension=0, tiled=True)
        right_lower = jnp.linalg.cholesky(lax.psum(inner(share, share), ("tok", "row")))
        piece = solve_lower(right_lower, share)
        right = lax.all_gather(piece, "row", axis=0, tiled=True)
    core = lax.psum(inner(back, jnp.dot(weight, right, precision=HIGH)), ("tok", "row"))
    return (math.sqrt(features) * left, math.sqrt(columns) * piece, core)


def split_rows(block):
    first = lax.reduce_precision(block, 8, 7)
    rest = block - first
    second = lax.reduce_precision(rest, 8, 7)
    third = rest - second
    return first.astype(BF16), second.astype(BF16), third.astype(BF16)


def product_kernel(first_ref, second_ref, third_ref, weight_ref, out_ref):
    weight = weight_ref[...]
    total = jnp.dot(third_ref[...], weight, preferred_element_type=F32)
    total += jnp.dot(second_ref[...], weight, preferred_element_type=F32)
    total += jnp.dot(first_ref[...], weight, preferred_element_type=F32)
    out_ref[0] = total


def applied_blocks(parts, weight, blocks):
    tokens, depth = parts[0].shape
    width = weight.shape[1] // blocks
    whole = pl.BlockSpec((tokens, depth), lambda i: (0, 0))
    return pl.pallas_call(
        product_kernel,
        grid=(blocks,),
        in_specs=[whole, whole, whole, pl.BlockSpec((depth, width), lambda i: (0, i))],
        out_specs=pl.BlockSpec((1, tokens, width), lambda i: (i, 0, 0)),
        out_shape=jax.ShapeDtypeStruct((blocks, tokens, width), F32),
        compiler_params=pltpu.CompilerParams(vmem_limit_bytes=48 * 2**20),
        cost_estimate=pl.CostEstimate(
            flops=6 * tokens * depth * weight.shape[1],
            bytes_accessed=4 * tokens * weight.shape[1] + 2 * weight.size,
            transcendentals=0,
        ),
    )(*parts, weight)


def inverse_factor(table):
    size = table.shape[0]
    nb = 64
    eye = (
        lax.broadcasted_iota(jnp.int32, (nb, nb), 0) == lax.broadcasted_iota(jnp.int32, (nb, nb), 1)
    ).astype(F32)
    index = lax.broadcasted_iota(jnp.int32, (8, 1), 0)
    for at in range(0, size, nb):
        work = jnp.concatenate([table[at : at + nb, at : at + nb], eye], axis=1)
        groups = [work[k : k + 8, :] for k in range(0, nb, 8)]
        for j in range(nb):
            own, place = divmod(j, 8)
            row = groups[own][place : place + 1, :]
            inverse = 1.0 / row[:, j : j + 1]
            for k in range(own, nb // 8):
                factor = groups[k][:, j : j + 1] * inverse
                if k == own:
                    factor = jnp.where(index > place, factor, 0.0)
                groups[k] = groups[k] - factor * row
        work = jnp.concatenate(groups, axis=0)
        pivots = jnp.sum(work[:, :nb] * eye, axis=1, keepdims=True)
        small = work[:, nb:] * lax.rsqrt(pivots)
        rows = jnp.dot(small, table[at : at + nb, :], precision=HIGH, preferred_element_type=F32)
        table[at : at + nb, :] = rows
        if at + nb < size:
            below = rows[:, at + nb : size]
            table[at + nb :, :] = table[at + nb :, :] - inner(below, rows)


def coefficient_kernel(gram_ref, square_ref, imaged_ref, left_ref, right_ref, core_ref, grams, now, table):
    tokens, size = imaged_ref.shape
    pltpu.sync_copy(gram_ref, grams.at[0])
    pltpu.sync_copy(square_ref, grams.at[1])
    now[...] = imaged_ref[...] / tokens
    eye = (
        lax.broadcasted_iota(jnp.int32, (size, size), 0)
        == lax.broadcasted_iota(jnp.int32, (size, size), 1)
    ).astype(F32)

    def one(i, carry):
        block = now[...]
        mapped = jnp.dot(grams[lax.rem(i, 2)], block, precision=HIGH, preferred_element_type=F32)
        table[:, :size] = inner(block, mapped)
        table[:, size:] = eye
        inverse_factor(table)
        inverse = table[:, size:]
        left_ref[...] = right_ref[...]
        right_ref[...] = outer(block, inverse)
        turned = outer(mapped, inverse)
        core_ref[...] = inner(block, turned)
        now[...] = turned / tokens
        return carry

    right_ref[...] = jnp.zeros_like(right_ref)
    lax.fori_loop(0, 2 * ITERS, one, 0)


def coefficients(gram, square, imaged):
    tokens, size = imaged.shape
    tall = jax.ShapeDtypeStruct((tokens, size), F32)
    vmem = pl.BlockSpec(memory_space=pltpu.VMEM)
    return pl.pallas_call(
        coefficient_kernel,
        in_specs=[pl.BlockSpec(memory_space=pl.ANY)] * 2 + [vmem],
        out_specs=[vmem] * 3,
        out_shape=[tall, tall, jax.ShapeDtypeStruct((size, size), F32)],
        scratch_shapes=[
            pltpu.VMEM((2, tokens, tokens), F32),
            pltpu.VMEM((tokens, size), F32),
            pltpu.VMEM((size, 2 * size), F32),
        ],
        compiler_params=pltpu.CompilerParams(vmem_limit_bytes=48 * 2**20),
    )(gram, square, imaged)


def token_space(hidden, resid, down_in, down_out, up_weight, start):
    blocks = lax.axis_size("row")
    tokens = hidden.shape[0] * lax.axis_size("tok")
    features = up_weight.shape[0] * blocks
    columns = up_weight.shape[1] * lax.axis_size("tok")
    width = up_weight.shape[1] // blocks
    own = lax.axis_index("row")

    code = lax.all_gather(jnp.dot(hidden, down_in, preferred_element_type=F32), "row")
    code = lax.all_gather(jnp.sum(code, axis=0), "tok", axis=0, tiled=True)
    base = lax.all_gather(resid.astype(F32), "tok", axis=0, tiled=True)
    acts = base + jnp.dot(code, down_out.astype(F32), precision=HIGH)
    gram = outer(acts, acts) / lax.axis_size("tok")

    parts = split_rows(acts)
    chunk = 256 if tokens % 256 == 0 else tokens
    pieces = []
    for at in range(0, tokens, chunk):
        block = applied_blocks([p[at : at + chunk] for p in parts], up_weight, blocks)
        pieces.append(lax.psum_scatter(block, "row", scatter_dimension=0, tiled=True)[0])
    applied = jnp.concatenate(pieces, axis=0)

    begin = lax.dynamic_slice_in_dim(start, own * width, width, axis=0).astype(F32)
    sums = jnp.concatenate(
        [gram, outer(applied, applied), jnp.dot(applied, begin, precision=HIGH)], axis=1
    )
    sums = lax.psum(sums, ("tok", "row"))
    gram, square, imaged = sums[:, :tokens], sums[:, tokens : 2 * tokens], sums[:, 2 * tokens :]

    left_coef, right_coef, core = coefficients(gram, square, imaged)
    left = inner(acts, left_coef)
    right = inner(applied, right_coef)
    return (math.sqrt(features) * left, math.sqrt(columns) * right, core)


def shards(hidden, *rest):
    tokens = hidden.shape[0] * lax.axis_size("tok")
    if tokens > 1024:
        return feature_space(hidden, *rest)
    return token_space(hidden, *rest)


def solution(mesh):
    placed = (
        P("tok", "row"),
        P("tok", "row"),
        P("row", None),
        P(None, "row"),
        P("row", "tok"),
        P("tok", None),
    )
    return jax.shard_map(
        shards,
        mesh=mesh,
        in_specs=placed,
        out_specs=(P("row", None), P(("tok", "row"), None), P()),
        check_vma=False,
    )
```
